32 devices in a mesh: row: 8 (over y, x, core), col: 4 (over z).
Axes of the slice: x: 2, y: 2, z: 4, core: 2. Of those that a mesh axis runs over, the one named last changes fastest.
Arguments:
- loads: float32 [3, 24576], P(None, 'row'), may hold values from -6 to 6
- nd_source: int32 [24576], P('row'), may hold values from 0 to 24575, as said below
- panel: bfloat16 [24576, 512], P('row', 'col'), as said below
- trailing: bfloat16 [24576, 24576], P('row', 'col'), may hold values from -6 to 6
- pattern: int32 [192, 192], P('row', 'col'), may hold values from 0 to 1
- owner: int32 [8], replicated, may hold values from 0 to 7, each once
Outputs:
- loads_out: float32 [3, 24576], P(None, 'row')
- trailing_out: bfloat16 [24576, 24576], P('row', 'col')
The draws below stay inside these ranges and needn't reach their ends.
Inputs may be any that keep to these rules, and one draw needn't show every extreme that they name: `nd_source`: a permutation; the rows t * 3072 to (t + 1) * 3072 - 1 take, from each block s of 3072 columns, exactly the columns s * 3072 + t * 384 to s * 3072 + (t + 1) * 384 - 1. `panel`: the 512 x 512 block at rows owner[0] * 3072 has a positive definite symmetric part. `owner`: a permutation of the row indices.
All inputs are finite; a program needn't handle non-finite values.
Results may differ from the reference program's by a relative error of at most 0.005.
Values may be sent and summed in bfloat16 or wider, within the bound.
A program may use at most 256 MiB of HBM per device.

```python
import math
import jax
import jax.numpy as jnp
from jax import lax

M = 24576
PIV = 512
BLK = 128
RD = 3072
Q = 384
N_ROW = 8


def draw_nd_source(key, part):
    target = jnp.arange(N_ROW, dtype=jnp.int32)[:, None]
    column = jnp.arange(RD, dtype=jnp.int32)[None, :]
    source_base = column // Q * RD + target * Q + column % Q
    key_list = jax.random.split(key, N_ROW)
    shuffle = jax.vmap(lambda subkey: jax.random.permutation(subkey, RD))(key_list)
    return jnp.take_along_axis(source_base, shuffle, axis=1).reshape(M).astype(jnp.int32)


def draw_panel(key, part):
    key_first, key_second = jax.random.split(jax.random.fold_in(key, 11))
    rows = jnp.arange(M, dtype=jnp.int32)[:, None]
    cols = jnp.arange(PIV, dtype=jnp.int32)[None, :]
    offset = rows % RD
    general = 0.3 * jax.random.normal(key_first, (M, PIV), jnp.float32)
    small = jax.random.uniform(key_second, (M, PIV), jnp.float32, -1.0, 1.0) * (1.5 / math.sqrt(PIV))
    diagonal = jnp.where(offset == cols, 3.0, 0.0)
    return jnp.where(offset < PIV, small + diagonal, general).astype(jnp.bfloat16)


def draw_pattern(key, part):
    key_first, key_second = jax.random.split(jax.random.fold_in(key, 23))
    count = M // BLK
    active = jax.random.randint(key_first, (count, 1), 0, 3) == 0
    filled = jax.random.randint(key_second, (count, count), 0, 2) == 1
    return (active & filled).astype(jnp.int32)


def levels(own_key, extent, cuts, smallest, high):
    def one(dim, blocks):
        steps = jax.random.uniform(jax.random.fold_in(jax.random.fold_in(own_key, 6), dim), (blocks,), jnp.float32, smallest / len(cuts), high / len(cuts))
        return jnp.repeat(jnp.exp(steps), extent[dim] // blocks).reshape((-1,) + (1,) * (len(extent) - dim - 1))

    loudness = one(*cuts[0])
    for cut in cuts[1:]:
        loudness = loudness * one(*cut)
    return loudness


def gaussian(rng, shape, spread, most, cuts=(), kind=jnp.bfloat16):
    values = jax.random.normal(rng, shape, jnp.float32) * spread
    if len(cuts) > 0:
        values = levels(rng, shape, cuts, -0.22, 0.18) * values
    return jnp.clip(values, min=-most, max=most).astype(kind)


def setup_inputs(seed: int = 0) -> dict:
    keys = jax.random.split(jax.random.key(seed), 7)
    return {
        "loads": gaussian(keys[0], (3, M), 1.0, 6.0, ((1, 8),), jnp.float32),
        "nd_source": draw_nd_source(jax.random.fold_in(keys[6], 71), 0),
        "panel": draw_panel(jax.random.fold_in(keys[6], 71), 0),
        "trailing": gaussian(keys[3], (M, M), 1.0, 6.0, ((0, 8), (1, 4))),
        "pattern": draw_pattern(jax.random.fold_in(keys[6], 71), 0),
        "owner": jax.random.permutation(keys[5], N_ROW).astype(jnp.int32),
    }


def reference(loads, nd_source, panel, trailing, pattern, owner):
    regrouped = jnp.take(loads, nd_source, axis=1)
    pivot_start = owner[0].astype(jnp.int32) * RD
    pivot_block = lax.dynamic_slice_in_dim(panel, pivot_start, PIV, 0).astype(jnp.float32)
    symmetric = 0.5 * (pivot_block + pivot_block.T)
    lower_factor = jnp.linalg.cholesky(symmetric)
    inverse = lax.linalg.triangular_solve(lower_factor, jnp.eye(PIV, dtype=jnp.float32), left_side=True, lower=True)
    inverse_half = inverse.astype(jnp.bfloat16)
    factor = jnp.dot(panel.astype(jnp.float32), inverse_half.T.astype(jnp.float32), preferred_element_type=jnp.float32).astype(jnp.bfloat16)
    pivot_loads = lax.dynamic_slice_in_dim(regrouped, pivot_start, PIV, 1)
    pivot_solve = jnp.dot(inverse, pivot_loads.T, precision=lax.Precision.HIGHEST)
    update = jnp.dot(factor.astype(jnp.float32), pivot_solve, precision=lax.Precision.HIGHEST).T
    positions = jnp.arange(M, dtype=jnp.int32)
    in_pivot = (positions >= pivot_start) & (positions < pivot_start + PIV)
    pivot_offset = jnp.clip(positions - pivot_start, 0, PIV - 1)
    loads_out = jnp.where(in_pivot[None, :], jnp.take(pivot_solve.T, pivot_offset, axis=1), regrouped - update)
    block_rows = RD // BLK
    block_cols = M // BLK

    def row_update(index):
        row_block = lax.dynamic_slice_in_dim(factor, index * RD, RD, 0)
        product = jnp.dot(row_block.astype(jnp.float32), factor.T.astype(jnp.float32), preferred_element_type=jnp.float32)
        old_rows = lax.dynamic_slice_in_dim(trailing, index * RD, RD, 0).astype(jnp.float32)
        flags = lax.dynamic_slice_in_dim(pattern, index * block_rows, block_rows, 0).astype(jnp.float32)
        masked = (product.reshape(block_rows, BLK, block_cols, BLK) * flags[:, None, :, None]).reshape(RD, M)
        return (old_rows - masked).astype(jnp.bfloat16)
    trailing_out = lax.map(row_update, jnp.arange(N_ROW, dtype=jnp.int32)).reshape(M, M)
    return (loads_out, trailing_out)
```

```python
import functools

import jax
import jax.numpy as jnp
from jax import lax
from jax.experimental import pallas as pl
from jax.experimental.pallas import tpu as pltpu
from jax.sharding import PartitionSpec as P

HIGHEST = lax.Precision.HIGHEST


def dot_nt(a, b, **kw):
    return lax.dot_general(a, b, (((1,), (1,)), ((), ())), preferred_element_type=jnp.float32, **kw)


def dot_nn(a, b, **kw):
    return lax.dot_general(a, b, (((1,), (0,)), ((), ())), preferred_element_type=jnp.float32, **kw)


def invert_block(d):
    nb = d.shape[0]
    rows = lax.broadcasted_iota(jnp.int32, (nb, nb), 0)
    cols = lax.broadcasted_iota(jnp.int32, (nb, nb), 1)
    w = (rows == cols).astype(jnp.float32)
    row_id = lax.broadcasted_iota(jnp.int32, (8, 1), 0)
    groups = nb // 8
    ds = [d[8 * g : 8 * g + 8] for g in range(groups)]
    ws = [w[8 * g : 8 * g + 8] for g in range(groups)]
    diag = (lax.broadcasted_iota(jnp.int32, (8, nb), 1), lax.broadcasted_iota(jnp.int32, (8, nb), 0))
    for k in range(nb - 1):
        g0 = k // 8
        row = ds[g0][k % 8 : k % 8 + 1]
        w_row = ws[g0][k % 8 : k % 8 + 1]
        inv = 1.0 / row[:, k : k + 1]
        row = row * inv
        w_row = w_row * inv
        for g in range(g0, groups):
            col = ds[g][:, k : k + 1]
            if g == g0:
                if k % 8 == 7:
                    continue
                col = jnp.where(row_id > k % 8, col, 0.0)
            ds[g] = ds[g] - col * row
            ws[g] = ws[g] - col * w_row
    out = []
    for g in range(groups):
        pivot = jnp.sum(jnp.where(diag[0] == diag[1] + 8 * g, ds[g], 0.0), axis=1, keepdims=True)
        out.append(ws[g] * lax.rsqrt(pivot))
    return jnp.concatenate(out, axis=0)


def factor_kernel(first, last, nb, a_in, w_in, a_ref, w_ref):
    n = a_in.shape[0]
    a_ref[...] = a_in[...]
    w_ref[...] = w_in[...]
    row_id = lax.broadcasted_iota(jnp.int32, (n, 1), 0)

    @pl.loop(first, last)
    def _(j):
        start = pl.multiple_of(j * nb, nb)
        here = pl.ds(start, nb)
        x = invert_block(a_ref[here, here])
        below = jnp.where(row_id >= start + nb, dot_nt(a_ref[:, here], x, precision=HIGHEST), 0.0)
        w_here = dot_nn(x, w_ref[here, :], precision=HIGHEST)
        w_ref[...] = w_ref[...] - dot_nn(below, w_here, precision=HIGHEST)
        w_ref[here, :] = w_here
        a_ref[...] = a_ref[...] - dot_nt(below, below, precision=HIGHEST)


def eliminate(a, w, first, last, nb):
    n = a.shape[0]
    shape = jax.ShapeDtypeStruct((n, n), jnp.float32)
    return pl.pallas_call(
        functools.partial(factor_kernel, first, last, nb),
        out_shape=(shape, shape),
        in_specs=[pl.BlockSpec(memory_space=pltpu.VMEM)] * 2,
        out_specs=[pl.BlockSpec(memory_space=pltpu.VMEM)] * 2,
        cost_estimate=pl.CostEstimate(flops=20_000_000_000, bytes_accessed=4 * n * n * 4, transcendentals=0),
        name="eliminate",
    )(a, w)


def trailing_kernel(block, chunk, flags, rows_ref, cols_ref, mask_ref, old_ref, new_ref):
    step = pl.program_id(0)
    tile, width = old_ref.shape
    for i in range(tile // block):
        here = pl.ds(i * block, block)
        block_row = step * (tile // block) + i

        @pl.loop(0, width // chunk)
        def _(j):
            there = pl.ds(pl.multiple_of(j * chunk, chunk), chunk)
            live = flags[block_row, j] != 0

            @pl.when(live)
            def _():
                product = dot_nt(rows_ref[here, :], cols_ref[there, :])
                mask = mask_ref[0, i : i + 1, there]
                new_ref[here, there] = (old_ref[here, there].astype(jnp.float32) - product * mask).astype(
                    new_ref.dtype
                )

            @pl.when(jnp.logical_not(live))
            def _():
                new_ref[here, there] = old_ref[here, there]


def update_trailing(trailing, factor_rows, factor_cols, pattern):
    height, width = trailing.shape
    depth = factor_rows.shape[1]
    block_rows, block_cols = pattern.shape
    block = height // block_rows
    per_tile = 2 if block_rows % 2 == 0 else 1
    tile = per_tile * block
    per_chunk = 8 if block_cols % 8 == 0 else 1
    chunk = per_chunk * block
    flags = jnp.max(pattern.reshape(block_rows, block_cols // per_chunk, per_chunk), axis=2)
    mask = jnp.broadcast_to(
        pattern.astype(jnp.float32)[:, :, None], (block_rows, block_cols, width // block_cols)
    ).reshape(block_rows // per_tile, per_tile, width)
    grid_spec = pltpu.PrefetchScalarGridSpec(
        num_scalar_prefetch=1,
        grid=(height // tile,),
        in_specs=[
            pl.BlockSpec((tile, depth), lambda i, f: (i, 0)),
            pl.BlockSpec((width, depth), lambda i, f: (0, 0), pipeline_mode=pl.Buffered(1)),
            pl.BlockSpec((1, per_tile, width), lambda i, f: (i, 0, 0)),
            pl.BlockSpec((tile, width), lambda i, f: (i, 0)),
        ],
        out_specs=pl.BlockSpec((tile, width), lambda i, f: (i, 0)),
    )
    return pl.pallas_call(
        functools.partial(trailing_kernel, block, chunk),
        grid_spec=grid_spec,
        out_shape=jax.ShapeDtypeStruct(trailing.shape, trailing.dtype),
        compiler_params=pltpu.CompilerParams(
            dimension_semantics=("arbitrary",), vmem_limit_bytes=40 * 1024 * 1024
        ),
        name="trailing",
    )(flags, factor_rows, factor_cols, mask, trailing)


def swap_add(array, axis):
    size = lax.axis_size(axis)
    bit = 1
    while bit < size:
        array = array + lax.ppermute(array, axis, [(i, i ^ bit) for i in range(size)])
        bit *= 2
    return array


def gather_columns(piece, axis):
    size = lax.axis_size(axis)
    me = lax.axis_index(axis)
    rows, width = piece.shape
    got = [piece]
    for shift in range(1, size):
        got.append(lax.ppermute(piece, axis, [(i, i ^ shift) for i in range(size)]))
    whole = jnp.zeros((rows, width * size), piece.dtype)
    for shift in range(size):
        whole = lax.dynamic_update_slice(whole, got[shift], (0, (me ^ shift) * width))
    return whole


def spread(panel_rows):
    row_count = lax.axis_size("row")
    col_count = lax.axis_size("col")
    holders = row_count // col_count
    group = lax.axis_index("row") // holders
    member = lax.axis_index("row") % holders
    away = group ^ lax.axis_index("col")
    bits = []
    bit = 1
    while bit < col_count:
        bits.append(bit)
        bit *= 2
    orders = [[bits[(m + t) % len(bits)] for t in range(len(bits))] for m in range(holders)]
    held = panel_rows
    for step in range(len(bits)):
        pairs = []
        takes = jnp.zeros((), jnp.bool_)
        for m in range(holders):
            span = sum(orders[m][:step])
            new = orders[m][step]
            for c in range(col_count):
                for q in range(col_count):
                    if (q ^ c) & ~span == 0:
                        source = (q * holders + m) * col_count + c
                        target = ((q ^ new) * holders + m) * col_count + c
                        pairs.append((source, target))
            takes = takes | ((member == m) & ((away & ~span) == new))
        came = lax.ppermute(held, ("row", "col"), pairs)
        held = jnp.where(takes, came, held)
    got = [held]
    for k in range(1, holders):
        got.append(lax.ppermute(held, "row", [(i, i ^ k) for i in range(row_count)]))
    pieces = []
    for j in range(holders):
        piece = got[0]
        for k in range(1, holders):
            piece = jnp.where((member ^ k) == j, got[k], piece)
        pieces.append(piece)
    return pieces


def per_device(loads, nd_source, panel, trailing, pattern, owner):
    row_dev = panel.shape[0]
    row_count = lax.axis_size("row")
    col_count = lax.axis_size("col")
    pivot_size = panel.shape[1] * col_count
    share_size = row_dev // row_count
    row_place = lax.axis_index("row")
    owner_row = owner[0]
    mine = row_place == owner_row

    piece = swap_add(jnp.where(mine, panel[:pivot_size], jnp.zeros((), panel.dtype)), "row")
    pivot_block = gather_columns(piece, "col").astype(jnp.float32)
    symmetric = 0.5 * (pivot_block + pivot_block.T)

    panel_rows = lax.all_gather(panel, "col", axis=1, tiled=True)

    nb = min(128, pivot_size)
    blocks = pivot_size // nb
    a, w = eliminate(symmetric, jnp.eye(pivot_size, dtype=jnp.float32), 0, blocks // 2, nb)
    a, w = eliminate(a, w, blocks // 2, blocks, nb)
    inverse = w
    inverse_half = inverse.astype(jnp.bfloat16)

    pieces = spread(panel_rows)

    arrived = lax.all_to_all(loads, "row", split_axis=1, concat_axis=1, tiled=True)
    source_slot = nd_source // row_dev * share_size + (nd_source % row_dev - row_place * share_size)
    regrouped = jnp.take(arrived, source_slot, axis=1)
    pivot_loads = lax.psum(jnp.where(mine, regrouped[:, :pivot_size], 0.0), "row")

    factor_rows = dot_nt(panel_rows, inverse_half).astype(jnp.bfloat16)
    pivot_solve = dot_nt(pivot_loads, inverse, precision=HIGHEST)
    update = dot_nt(pivot_solve, factor_rows.astype(jnp.float32), precision=HIGHEST)
    plain = regrouped - update
    head = jnp.where(mine, pivot_solve, plain[:, :pivot_size])
    loads_out = jnp.concatenate([head, plain[:, pivot_size:]], axis=1)

    factor_cols = jnp.concatenate(
        [dot_nt(piece, inverse_half).astype(jnp.bfloat16) for piece in pieces], axis=0
    )
    trailing_out = update_trailing(trailing, factor_rows, factor_cols, pattern)
    return (loads_out, trailing_out)


def solution(mesh):
    return jax.shard_map(
        per_device,
        mesh=mesh,
        in_specs=(P(None, "row"), P("row"), P("row", "col"), P("row", "col"), P("row", "col"), P()),
        out_specs=(P(None, "row"), P("row", "col")),
        check_vma=False,
    )
```
